32 devices in a mesh: row: 8 (over y, x, core), col: 4 (over z).
Axes of the slice: x: 2, y: 2, z: 4, core: 2. Of those that a mesh axis runs over, the one named last changes fastest.
Arguments:
- mode_block: float32 [32768, 256], P(('row', 'col')), may hold values from -80 to 80
- k_blocks: float32 [256, 3, 128, 128], P(('row', 'col')), may hold values from -1 to 9
- block_cols: int32 [256, 3], P(('row', 'col')), may hold values from 0 to 255, as said below
- panel_node: int32 [4096], replicated, may hold values from 0 to 32767, as said below
- added_mass: bfloat16 [4096, 4096], P('row', 'col'), may hold values from -0.125 to 0.125
- low_edge: int32 [256], replicated, may hold values from 4 to 8
- high_edge: int32 [256], replicated, may hold values from 40 to 56
Outputs:
- filtered: float32 [32768, 256], P(('row', 'col'))
The draws below stay inside these ranges and needn't reach their ends.
Inputs may be any that keep to these rules, and one draw needn't show every extreme that they name: `panel_node`: distinct shell rows. Cut the panels into 32 aligned blocks of 128; in each block at most 8 panels lie on the 1024 rows of one shell device (rows d * 1024 to (d + 1) * 1024 - 1), exactly 8 for some device, and the panels of a block on one device are consecutive. `block_cols`: row i holds i first, then two different block rows among i - 2 to i + 2 other than i.
All inputs are finite; a program needn't handle non-finite values.
Results may differ from the reference program's by a relative error of at most 0.0015.
Values may be sent and summed in bfloat16 or wider, within the bound.
A program may use at most 64 MiB of HBM per device.

```python
import jax
import jax.numpy as jnp
from jax import lax

NB = 256
BLK = 128
KB = 3
DEGREE = 3
OUTER = 2
ROWS_DEV = 1024
PB = 128
NS = 32768
NP = 4096
DEVICES = 32


def wet_layout(key):
    hull_key, swap_key, spot_key, perm_key = jax.random.split(key, 4)
    spread = (PB + DEVICES - 1) // DEVICES
    capacity = 2 * spread
    heavy_count = max(1, PB // (4 * spread))
    boundary = heavy_count * capacity
    within = jnp.arange(PB)
    position = jnp.where(within < boundary, within // capacity, heavy_count + (within - boundary) // spread)
    offset = jnp.where(within < boundary, within % capacity, (within - boundary) % spread)
    hull_order = jax.random.permutation(hull_key, DEVICES)
    device_order = jnp.tile(hull_order[None, :], (DEVICES, 1))
    heavy_spot = jax.random.randint(swap_key, (DEVICES,), 0, heavy_count)
    second = jax.random.randint(spot_key, (DEVICES,), 0, DEVICES)
    blocks = jnp.arange(DEVICES)
    heavy_value = device_order[blocks, heavy_spot]
    second_value = device_order[blocks, second]
    device_order = device_order.at[blocks, heavy_spot].set(second_value)
    device_order = device_order.at[blocks, second].set(heavy_value)
    source = device_order[:, position]
    counts = jnp.sum((source[:, :, None] == jnp.arange(DEVICES)[None, None, :]).astype(jnp.int32), axis=1)
    before = jnp.cumsum(counts, axis=0) - counts
    base_rank = jnp.take_along_axis(before, source, axis=1)
    rank_on_device = base_rank + offset[None, :]
    row_perms = jax.vmap(lambda sub_key: jax.random.permutation(sub_key, ROWS_DEV))(jax.random.split(perm_key, DEVICES))
    row_pick = row_perms[source, rank_on_device]
    return (source * ROWS_DEV + row_pick).reshape(-1).astype(jnp.int32)


def draw_panel_node(key, part):
    return wet_layout(jax.random.fold_in(key, 7))


def draw_block_cols(key, part):
    block_total = NS // BLK
    index_rows = jnp.arange(block_total)
    offsets = jnp.array([-2, -1, 1, 2], dtype=jnp.int32)
    candidate = index_rows[:, None] + offsets[None, :]
    valid = (candidate >= 0) & (candidate < block_total)
    scores = jax.random.randint(key, (block_total, 4), 0, 1000) * 4 + jnp.arange(4)[None, :]
    scores = jnp.where(valid, scores, 100000)
    top_values, picked = lax.top_k(-scores, 2)
    chosen = jnp.take_along_axis(candidate, picked, axis=1)
    return jnp.concatenate([index_rows[:, None], chosen], axis=1).astype(jnp.int32)


def draw_k_blocks(key, part):
    noise_key, diag_key = jax.random.split(key, 2)
    block_shape = (NS // BLK, KB, BLK, BLK)
    values = jnp.clip(jax.random.normal(noise_key, block_shape, jnp.float32), -6.0, 6.0)
    values = values * (KB * BLK) ** (-0.5)
    diagonal = jnp.exp(jax.random.uniform(diag_key, (NS // BLK, BLK), jnp.float32, jnp.log(2.0), jnp.log(8.0)))
    identity = jnp.eye(BLK, dtype=jnp.float32)
    return values.at[:, 0].add(diagonal[:, :, None] * identity[None, :, :])


def draw_mode_block(key, part):
    base_key, row_key, col_key = jax.random.split(key, 3)
    base = jnp.clip(jax.random.normal(base_key, (NS, NB), jnp.float32), -6.0, 6.0)
    ramp = jnp.exp(jnp.log(3.0) * jnp.arange(NS).astype(jnp.float32) / NS)[:, None]
    row_scale = jnp.exp(jax.random.uniform(row_key, (NS, 1), jnp.float32, 0.0, jnp.log(10.0))) * ramp
    col_scale = jnp.exp(jax.random.uniform(col_key, (1, NB), jnp.float32, 0.0, jnp.log(10.0)))
    return base * row_scale * col_scale / 30.0


def place_ends(values, key, smallest, largest):
    spot = [jax.random.randint(jax.random.fold_in(key, axis), (), 0, length) for axis, length in enumerate(values.shape)]
    longest = values.shape.index(max(values.shape))
    neighbour = spot[:longest] + [(spot[longest] + 1) % values.shape[longest]] + spot[longest + 1:]
    return values.at[tuple(spot)].set(smallest).at[tuple(neighbour)].set(largest)


def strengthened(result, stream_key, source, target, blocks, factor):
    def block_of(axis_at):
        return (jnp.arange(result.shape[axis_at]) // (result.shape[axis_at] // blocks)).reshape((-1,) + (1,) * (result.ndim - 1 - axis_at))

    one_side = jax.random.permutation(stream_key, blocks)[block_of(target)]
    far = (block_of(target) + blocks // 2) % blocks
    return jnp.where((block_of(source) == one_side) | (block_of(source) == far), factor * result, result)


def level_of(own_key, shape, pieces, least, largest):
    factor_of, own = 1.0, jax.random.fold_in(own_key, 6)
    for dim, blocks in pieces:
        draws = jnp.exp(jax.random.uniform(jax.random.fold_in(own, dim), (blocks,), jnp.float32, least / len(pieces), largest / len(pieces)))
        factor_of = factor_of * jnp.repeat(draws, shape[dim] // blocks).reshape([-1 if axis == dim else 1 for axis in range(len(shape))])
    return factor_of


def bell_draw_with(stream_key, shape, deviation, most, pieces, heavy, kind=jnp.bfloat16):
    values = deviation * jax.random.normal(stream_key, shape, jnp.float32)
    if pieces:
        values = values * level_of(stream_key, shape, pieces, -0.22, 0.18)
    return jnp.clip(strengthened(values, jax.random.fold_in(stream_key, 3), *heavy), -most, most).astype(kind)


def setup_inputs(seed: int = 0) -> dict:
    seeds = jax.random.split(jax.random.key(seed), 8)
    return {
        "mode_block": draw_mode_block(jax.random.fold_in(seeds[7], 71), 0),
        "k_blocks": draw_k_blocks(jax.random.fold_in(seeds[7], 71), 0),
        "block_cols": draw_block_cols(jax.random.fold_in(seeds[7], 71), 0),
        "panel_node": draw_panel_node(jax.random.fold_in(seeds[7], 71), 0),
        "added_mass": bell_draw_with(seeds[4], (NP, NP), NP ** -0.5, 0.125, ((0, 8), (1, 4)), (1, 0, 8, 2.0)),
        "low_edge": place_ends(jax.random.randint(seeds[5], (NB,), 4, 9), jax.random.fold_in(seeds[5], 1), 4, 8).astype(jnp.int32),
        "high_edge": place_ends(jax.random.randint(seeds[6], (NB,), 40, 57), jax.random.fold_in(seeds[6], 1), 40, 56).astype(jnp.int32),
    }


def stiffness(vectors, k_blocks, block_cols):
    row_total = k_blocks.shape[0]
    block_size = k_blocks.shape[2]
    blocked = vectors.reshape(row_total, block_size, vectors.shape[1])

    def one_row(paired):
        values, columns = paired
        chosen = blocked[columns]
        return jnp.einsum('kij,kjn->in', values, chosen, precision=lax.Precision.HIGHEST)
    return lax.map(one_row, (k_blocks, block_cols)).reshape(vectors.shape)

def operate(vectors, k_blocks, block_cols, panel_node, added_mass):
    wetted = vectors[panel_node].astype(jnp.bfloat16)
    pressure = jnp.dot(added_mass, wetted, preferred_element_type=jnp.float32)
    loads = jnp.zeros_like(vectors).at[panel_node].set(pressure)
    return stiffness(vectors, k_blocks, block_cols) + loads

def reference(mode_block, k_blocks, block_cols, panel_node, added_mass, low_edge, high_edge):
    lower = low_edge.astype(jnp.float32) * 0.25
    upper = high_edge.astype(jnp.float32) * 0.25
    centre = 0.5 * (upper + lower)
    radius = 0.5 * (upper - lower)
    current = mode_block
    for outer_no in range(OUTER):
        previous = current
        image = operate(current, k_blocks, block_cols, panel_node, added_mass)
        current = (image - centre * current) / radius
        for degree_no in range(DEGREE - 1):
            image = operate(current, k_blocks, block_cols, panel_node, added_mass)
            following = 2.0 * (image - centre * current) / radius - previous
            previous = current
            current = following
        squares = lax.optimization_barrier(jnp.sum(current * current, axis=0))
        current = current / jnp.sqrt(squares / NS + 1e-06)
    return current
```

```python
import functools

import jax
import jax.numpy as jnp
from jax import lax
from jax.experimental import pallas as pl
from jax.experimental.pallas import tpu as pltpu
from jax.sharding import PartitionSpec as P

DEGREE = 3
OUTER = 2
SUBLANES = 8
MESH = pl.DeviceIdType.MESH


def dot(left, right):
    return jnp.dot(left, right, preferred_element_type=jnp.float32)


def split(value):
    high = value.astype(jnp.bfloat16)
    low = (value - high.astype(jnp.float32)).astype(jnp.bfloat16)
    return high, low


def one_hot(left, right):
    return jnp.where(left == right, 1.0, 0.0).astype(jnp.bfloat16)


def kernel(
    n_row, n_col,
    rel_ref, start_ref, k_ref, send_ref, back_ref, in_ref, out_code_ref, mass_ref,
    centre_ref, inverse_ref, result_ref,
    cur, prev, v_hi, v_lo, stiff, k_hi, k_lo, pick, place, order_in, order_out,
    disp_out, disp_in, wet, partial, rs_out, rs_in, ret_out, ret_in, halo, sq_out, sq_in,
    halo_send, halo_recv, disp_send, disp_recv, wet_send, wet_recv,
    rs_send, rs_recv, ret_send, ret_recv, sq_send, sq_recv,
):
    n_dev = n_row * n_col
    my_row = lax.axis_index("row")
    my_col = lax.axis_index("col")
    me = my_row * n_col + my_col
    rows, width = cur.shape
    slots = disp_out.shape[1]
    flat = n_dev * slots
    block = k_ref.shape[2]
    pair = 2 * block
    pairs = rows // pair
    per_block = order_in.shape[0]

    def device(index):
        return (index // n_col, lax.rem(index, n_col))

    barrier = pltpu.get_barrier_semaphore()

    def greet(k, carry):
        pl.semaphore_signal(
            barrier, inc=1, device_id=device(lax.rem(me + k, n_dev)), device_id_type=MESH
        )
        return carry

    lax.fori_loop(1, n_dev, greet, 0)

    shape = (flat, rows)
    pick[...] = one_hot(send_ref[...], lax.broadcasted_iota(jnp.int32, shape, 1))
    place[...] = one_hot(lax.broadcasted_iota(jnp.int32, (rows, flat), 0), back_ref[...])
    order_in[...] = one_hot(in_ref[...], lax.broadcasted_iota(jnp.int32, (per_block, flat), 1))
    order_out[...] = one_hot(
        lax.broadcasted_iota(jnp.int32, (flat, per_block), 0), out_code_ref[...]
    )
    cur[...] = start_ref[...]
    prev[...] = start_ref[...]
    pl.semaphore_wait(barrier, n_dev - 1)

    def exchange(source, target, send, recv, k, whole):
        to = lax.rem(me + k, n_dev)
        return pltpu.make_async_remote_copy(
            src_ref=source if whole else source.at[to],
            dst_ref=target.at[me],
            send_sem=send.at[k],
            recv_sem=recv.at[k],
            device_id=device(to),
            device_id_type=MESH,
        )

    def start_all(source, target, send, recv, whole=False):
        def step(k, carry):
            exchange(source, target, send, recv, k, whole).start()
            return carry

        lax.fori_loop(1, n_dev, step, 0)

    def wait_all(source, target, send, recv, whole=False):
        def step(k, carry):
            exchange(source, target, send, recv, k, whole).wait()
            return carry

        lax.fori_loop(1, n_dev, step, 0)

    def wet_copy(k):
        return pltpu.make_async_remote_copy(
            src_ref=wet.at[my_row],
            dst_ref=wet.at[my_row],
            send_sem=wet_send.at[k],
            recv_sem=wet_recv.at[k],
            device_id=(lax.rem(my_row + k, n_row), my_col),
            device_id_type=MESH,
        )

    def rs_copy(k):
        to = lax.rem(my_col + k, n_col)
        return pltpu.make_async_remote_copy(
            src_ref=rs_out.at[to],
            dst_ref=rs_in.at[my_col],
            send_sem=rs_send.at[k],
            recv_sem=rs_recv.at[k],
            device_id=(my_row, to),
            device_id_type=MESH,
        )

    def halo_copy(side, slot):
        source = cur.at[pl.ds(rows - pair, pair)] if side == 0 else cur.at[pl.ds(0, pair)]
        to = lax.rem(me + (1 if side == 0 else n_dev - 1), n_dev)
        return pltpu.make_async_remote_copy(
            src_ref=source,
            dst_ref=halo.at[slot, side],
            send_sem=halo_send.at[side],
            recv_sem=halo_recv.at[slot, side],
            device_id=device(to),
            device_id_type=MESH,
        )

    def banded(q, first, values_hi, values_lo):
        count = values_hi.shape[0]
        window_hi = k_hi[q, :, first : first + count]
        window_lo = k_lo[q, :, first : first + count]
        return (
            dot(window_hi, values_hi) + dot(window_lo, values_hi) + dot(window_hi, values_lo)
        )

    def build_band():
        for q in range(pairs):
            for half in range(2):
                i = 2 * q + half
                for o in range(6):
                    total = jnp.zeros((block, block), jnp.float32)
                    for k in range(k_ref.shape[1]):
                        flag = (rel_ref[i, k] == o).astype(jnp.float32)
                        total = total + k_ref[i, k] * flag
                    high, low = split(total)
                    k_hi[q, half * block : (half + 1) * block, o * block : (o + 1) * block] = high
                    k_lo[q, half * block : (half + 1) * block, o * block : (o + 1) * block] = low

    def operate(step_no, degree_no):
        slot = lax.rem(step_no, 2)
        high, low = split(cur[...])
        v_hi[...] = high
        v_lo[...] = low
        chosen = dot(pick[...], v_hi[...])
        disp_out[...] = chosen.reshape(n_dev, slots, width).astype(jnp.bfloat16)
        start_all(disp_out, disp_in, disp_send, disp_recv)
        for side in range(2):
            halo_copy(side, slot).start()
        disp_in[me] = disp_out[me]

        @pl.when(step_no == 0)
        def _():
            build_band()

        for q in range(pairs):
            first = max(q - 1, 0) * pair
            last = min(q + 2, pairs) * pair
            stiff[q * pair : (q + 1) * pair, :] = banded(
                q, pair if q == 0 else 0, v_hi[first:last, :], v_lo[first:last, :]
            )
        wait_all(disp_out, disp_in, disp_send, disp_recv)
        arrived = disp_in[...].astype(jnp.float32).reshape(flat, width).astype(jnp.bfloat16)
        wet[my_row] = dot(order_in[...], arrived).astype(jnp.bfloat16)
        for k in range(1, n_row):
            wet_copy(k).start()
        for k in range(1, n_row):
            wet_copy(k).wait()
        partial[...] = dot(mass_ref[...], wet[...].reshape(n_row * per_block, width))
        rs_out[...] = partial[...].reshape(n_col, per_block, width).astype(jnp.bfloat16)
        for k in range(1, n_col):
            rs_copy(k).start()
        pressure = partial[pl.ds(pl.multiple_of(my_col * per_block, per_block), per_block), :]
        for k in range(1, n_col):
            rs_copy(k).wait()
        for k in range(1, n_col):
            pressure = pressure + rs_in[lax.rem(my_col + k, n_col)].astype(jnp.float32)
        high, low = split(pressure)
        ret_out[...] = (dot(order_out[...], high) + dot(order_out[...], low)).reshape(
            n_dev, slots, width
        )
        start_all(ret_out, ret_in, ret_send, ret_recv)
        ret_in[me] = ret_out[me]
        for side in range(2):
            halo_copy(side, slot).wait()
        high, low = split(halo[slot, 0])
        stiff[0:pair, :] += banded(0, 0, high, low)
        high, low = split(halo[slot, 1])
        stiff[rows - pair : rows, :] += banded(pairs - 1, 2 * pair, high, low)
        wait_all(ret_out, ret_in, ret_send, ret_recv)
        high, low = split(ret_in[...].reshape(flat, width))
        image = stiff[...] + (dot(place[...], high) + dot(place[...], low))
        alpha = jnp.where(degree_no == 0, 1.0, 2.0).astype(jnp.float32)
        beta = jnp.where(degree_no == 0, 0.0, 1.0).astype(jnp.float32)
        now = cur[...]
        following = (image - centre_ref[...] * now) * (alpha * inverse_ref[...]) - beta * prev[...]
        prev[...] = now
        cur[...] = following

    def filter_pass(outer_no, carry):
        def degree_step(degree_no, inner):
            operate(outer_no * DEGREE + degree_no, degree_no)
            return inner

        lax.fori_loop(0, DEGREE, degree_step, 0)
        now = cur[...]
        sq_out[...] = jnp.sum(now * now, axis=0, keepdims=True)
        target = sq_in.at[outer_no]
        start_all(sq_out, target, sq_send, sq_recv, True)
        sq_in[outer_no, me] = sq_out[...]
        wait_all(sq_out, target, sq_send, sq_recv, True)
        squares = jnp.sum(sq_in[outer_no], axis=0)
        scaled = now / jnp.sqrt(squares / (rows * n_dev) + 1e-06)
        cur[...] = scaled
        prev[...] = scaled
        return carry

    lax.fori_loop(0, OUTER, filter_pass, 0)
    result_ref[...] = cur[...]


def body(mode_block, k_blocks, block_cols, panel_node, added_mass, low_edge, high_edge):
    n_row = lax.axis_size("row")
    n_col = lax.axis_size("col")
    devices = n_row * n_col
    my_row = lax.axis_index("row")
    my_col = lax.axis_index("col")
    linear = my_row * n_col + my_col
    rows_dev, width = mode_block.shape
    block_size = k_blocks.shape[2]
    blocks_dev = rows_dev // block_size
    per_block = panel_node.shape[0] // devices
    most = 2 * ((per_block + devices - 1) // devices)
    slots = (most + SUBLANES - 1) // SUBLANES * SUBLANES
    flat = devices * slots

    panel_rows = panel_node.reshape(devices, per_block)
    source = panel_rows // rows_dev
    within = jnp.arange(per_block)
    earlier = within[None, :] < within[:, None]
    owned = source == linear
    rank = jnp.sum((owned[:, None, :] & earlier[None]).astype(jnp.int32), axis=2)
    hit = owned[:, None, :] & (rank[:, None, :] == jnp.arange(slots)[None, :, None])
    local = panel_rows - linear * rows_dev + 1
    back = jnp.sum(jnp.where(hit, local[:, None, :], 0), axis=2) - 1
    send = back.reshape(n_col, n_row, slots).transpose(1, 0, 2)

    def codes(index):
        mine = lax.dynamic_index_in_dim(source, index, 0, keepdims=False)
        same = mine[:, None] == mine[None, :]
        return mine * slots + jnp.sum((same & earlier).astype(jnp.int32), axis=1)

    in_code = codes(my_col * n_row + my_row)
    out_code = codes(linear)
    pair_base = jnp.arange(blocks_dev)[:, None] // 2 * 2
    relative = block_cols - (linear * blocks_dev - 2) - pair_base

    lower = low_edge.astype(jnp.float32) * 0.25
    upper = high_edge.astype(jnp.float32) * 0.25
    centre = (0.5 * (upper + lower)).reshape(1, width)
    inverse = (1.0 / (0.5 * (upper - lower))).reshape(1, width)

    pair = 2 * block_size
    pairs = rows_dev // pair
    f32, bf16 = jnp.float32, jnp.bfloat16
    vmem = pl.BlockSpec(memory_space=pltpu.VMEM)
    dma = pltpu.SemaphoreType.DMA
    return pl.pallas_call(
        functools.partial(kernel, n_row, n_col),
        out_shape=jax.ShapeDtypeStruct(mode_block.shape, f32),
        in_specs=[pl.BlockSpec(memory_space=pltpu.SMEM)] + [vmem] * 9,
        out_specs=vmem,
        scratch_shapes=[
            pltpu.VMEM((rows_dev, width), f32),
            pltpu.VMEM((rows_dev, width), f32),
            pltpu.VMEM((rows_dev, width), bf16),
            pltpu.VMEM((rows_dev, width), bf16),
            pltpu.VMEM((rows_dev, width), f32),
            pltpu.VMEM((pairs, pair, 3 * pair), bf16),
            pltpu.VMEM((pairs, pair, 3 * pair), bf16),
            pltpu.VMEM((flat, rows_dev), bf16),
            pltpu.VMEM((rows_dev, flat), bf16),
            pltpu.VMEM((per_block, flat), bf16),
            pltpu.VMEM((flat, per_block), bf16),
            pltpu.VMEM((devices, slots, width), bf16),
            pltpu.VMEM((devices, slots, width), bf16),
            pltpu.VMEM((n_row, per_block, width), bf16),
            pltpu.VMEM((n_col * per_block, width), f32),
            pltpu.VMEM((n_col, per_block, width), bf16),
            pltpu.VMEM((n_col, per_block, width), bf16),
            pltpu.VMEM((devices, slots, width), f32),
            pltpu.VMEM((devices, slots, width), f32),
            pltpu.VMEM((2, 2, pair, width), f32),
            pltpu.VMEM((1, width), f32),
            pltpu.VMEM((OUTER, devices, 1, width), f32),
            dma((2,)),
            dma((2, 2)),
            dma((devices,)),
            dma((devices,)),
            dma((n_row,)),
            dma((n_row,)),
            dma((n_col,)),
            dma((n_col,)),
            dma((devices,)),
            dma((devices,)),
            dma((devices,)),
            dma((devices,)),
        ],
        compiler_params=pltpu.CompilerParams(
            collective_id=0, has_side_effects=True, vmem_limit_bytes=60 * 1024 * 1024
        ),
    )(
        relative,
        mode_block,
        k_blocks,
        send.reshape(flat, 1),
        back.reshape(1, flat),
        in_code.reshape(per_block, 1),
        out_code.reshape(1, per_block),
        added_mass,
        centre,
        inverse,
    )


def solution(mesh):
    placed = (
        P(("row", "col"), None),
        P(("row", "col"), None, None, None),
        P(("row", "col"), None),
        P(),
        P("row", "col"),
        P(),
        P(),
    )
    return jax.shard_map(
        body, mesh=mesh, in_specs=placed, out_specs=P(("row", "col"), None), check_vma=False
    )
```

```python
import functools

import jax
import jax.numpy as jnp
from jax import lax
from jax.experimental import pallas as pl
from jax.experimental.pallas import tpu as pltpu
from jax.sharding import PartitionSpec as P

DEGREE = 3
OUTER = 2
SUBLANES = 8
PACKED = 16
CODE_BITS = 15.0
MESH = pl.DeviceIdType.MESH


def dot(left, right):
    return jnp.dot(left, right, preferred_element_type=jnp.float32)


def split(value):
    high = value.astype(jnp.bfloat16)
    low = (value - high.astype(jnp.float32)).astype(jnp.bfloat16)
    return high, low


def encode(value):
    largest = jnp.maximum(jnp.max(jnp.abs(value), axis=0, keepdims=True), 1e-30)
    power = jnp.ceil(jnp.log2(largest))
    coded = jnp.clip(jnp.round(value * jnp.exp2(CODE_BITS - power)), -32767.0, 32767.0)
    powers = jnp.broadcast_to(power, (PACKED, value.shape[1]))
    return coded.astype(jnp.int32).astype(jnp.int16), powers.astype(jnp.int32).astype(jnp.int16)


def decode(coded, powers):
    power = powers.astype(jnp.int32).astype(jnp.float32)[0:1]
    return coded.astype(jnp.int32).astype(jnp.float32) * jnp.exp2(power - CODE_BITS)


def one_hot(left, right):
    return jnp.where(left == right, 1.0, 0.0).astype(jnp.bfloat16)


def kernel(
    n_row, n_col,
    rel_ref, start_ref, k_ref, send_ref, back_ref, in_ref, out_code_ref, mass_ref,
    centre_ref, inverse_ref, result_ref,
    cur, prev, v_hi, v_lo, stiff, k_hi, k_lo, pick, place, order_in, order_out,
    disp_out, disp_in, wet, partial, rs_out, rs_in, ret_out, ret_in, halo_out, halo, sq_out, sq_in,
    halo_send, halo_recv, disp_send, disp_recv, wet_send, wet_recv,
    rs_send, rs_recv, ret_send, ret_recv, sq_send, sq_recv,
):
    n_dev = n_row * n_col
    my_row = lax.axis_index("row")
    my_col = lax.axis_index("col")
    me = my_row * n_col + my_col
    rows, width = cur.shape
    slots = disp_out.shape[1]
    flat = n_dev * slots
    block = k_ref.shape[2]
    pair = 2 * block
    pairs = rows // pair
    per_block = order_in.shape[0]

    def device(index):
        return (index // n_col, lax.rem(index, n_col))

    barrier = pltpu.get_barrier_semaphore()

    def greet(k, carry):
        pl.semaphore_signal(
            barrier, inc=1, device_id=device(lax.rem(me + k, n_dev)), device_id_type=MESH
        )
        return carry

    lax.fori_loop(1, n_dev, greet, 0)

    shape = (flat, rows)
    pick[...] = one_hot(send_ref[...], lax.broadcasted_iota(jnp.int32, shape, 1))
    place[...] = one_hot(lax.broadcasted_iota(jnp.int32, (rows, flat), 0), back_ref[...])
    order_in[...] = one_hot(in_ref[...], lax.broadcasted_iota(jnp.int32, (per_block, flat), 1))
    order_out[...] = one_hot(
        lax.broadcasted_iota(jnp.int32, (flat, per_block), 0), out_code_ref[...]
    )
    cur[...] = start_ref[...]
    prev[...] = start_ref[...]
    pl.semaphore_wait(barrier, n_dev - 1)

    def exchange(source, target, send, recv, k, whole):
        to = lax.rem(me + k, n_dev)
        return pltpu.make_async_remote_copy(
            src_ref=source if whole else source.at[to],
            dst_ref=target.at[me],
            send_sem=send.at[k],
            recv_sem=recv.at[k],
            device_id=device(to),
            device_id_type=MESH,
        )

    def start_all(source, target, send, recv, whole=False):
        def step(k, carry):
            exchange(source, target, send, recv, k, whole).start()
            return carry

        lax.fori_loop(1, n_dev, step, 0)

    def wait_all(source, target, send, recv, whole=False):
        def step(k, carry):
            exchange(source, target, send, recv, k, whole).wait()
            return carry

        lax.fori_loop(1, n_dev, step, 0)

    chips = n_row // 2
    partner = my_row + 1 - 2 * lax.rem(my_row, 2)

    def wet_copy(k):
        return pltpu.make_async_remote_copy(
            src_ref=wet.at[my_row],
            dst_ref=wet.at[my_row],
            send_sem=wet_send.at[k],
            recv_sem=wet_recv.at[k],
            device_id=(lax.rem(my_row + 2 * k, n_row), my_col),
            device_id_type=MESH,
        )

    def wet_forward(k):
        held = wet.at[lax.rem(my_row + n_row - 2 * k, n_row)]
        return pltpu.make_async_remote_copy(
            src_ref=held,
            dst_ref=held,
            send_sem=wet_send.at[chips + k],
            recv_sem=wet_recv.at[chips + k],
            device_id=(partner, my_col),
            device_id_type=MESH,
        )

    def rs_copy(k):
        to = lax.rem(my_col + k, n_col)
        return pltpu.make_async_remote_copy(
            src_ref=rs_out.at[to],
            dst_ref=rs_in.at[my_col],
            send_sem=rs_send.at[k],
            recv_sem=rs_recv.at[k],
            device_id=(my_row, to),
            device_id_type=MESH,
        )

    def halo_copy(side, slot):
        to = lax.rem(me + (1 if side == 0 else n_dev - 1), n_dev)
        return pltpu.make_async_remote_copy(
            src_ref=halo_out.at[side],
            dst_ref=halo.at[slot, side],
            send_sem=halo_send.at[side],
            recv_sem=halo_recv.at[slot, side],
            device_id=device(to),
            device_id_type=MESH,
        )

    def banded(q, first, values_hi, values_lo):
        count = values_hi.shape[0]
        window_hi = k_hi[q, :, first : first + count]
        window_lo = k_lo[q, :, first : first + count]
        return (
            dot(window_hi, values_hi) + dot(window_lo, values_hi) + dot(window_hi, values_lo)
        )

    def build_band():
        for q in range(pairs):
            for half in range(2):
                i = 2 * q + half
                for o in range(6):
                    total = jnp.zeros((block, block), jnp.float32)
                    for k in range(k_ref.shape[1]):
                        flag = (rel_ref[i, k] == o).astype(jnp.float32)
                        total = total + k_ref[i, k] * flag
                    high, low = split(total)
                    k_hi[q, half * block : (half + 1) * block, o * block : (o + 1) * block] = high
                    k_lo[q, half * block : (half + 1) * block, o * block : (o + 1) * block] = low

    def operate(step_no, degree_no):
        slot = lax.rem(step_no, 2)
        high, low = split(cur[...])
        v_hi[...] = high
        v_lo[...] = low
        chosen = dot(pick[...], v_hi[...])
        disp_out[...] = chosen.reshape(n_dev, slots, width).astype(jnp.bfloat16)
        start_all(disp_out, disp_in, disp_send, disp_recv)
        for side in range(2):
            edge = cur[rows - pair : rows, :] if side == 0 else cur[0:pair, :]
            coded, powers = encode(edge)
            halo_out[side, 0:pair, :] = coded
            halo_out[side, pair : pair + PACKED, :] = powers
        disp_in[me] = disp_out[me]

        @pl.when(step_no == 0)
        def _():
            build_band()

        for q in range(pairs):
            first = max(q - 1, 0) * pair
            last = min(q + 2, pairs) * pair
            stiff[q * pair : (q + 1) * pair, :] = banded(
                q, pair if q == 0 else 0, v_hi[first:last, :], v_lo[first:last, :]
            )
        wait_all(disp_out, disp_in, disp_send, disp_recv)
        arrived = disp_in[...].astype(jnp.float32).reshape(flat, width).astype(jnp.bfloat16)
        wet[my_row] = dot(order_in[...], arrived).astype(jnp.bfloat16)
        for k in range(1, chips):
            wet_copy(k).start()
        wet_forward(0).start()
        for side in range(2):
            halo_copy(side, slot).start()
        for k in range(1, chips):
            wet_copy(k).wait_recv()
            wet_forward(k).start()
        for k in range(1, chips):
            wet_copy(k).wait_send()
        for k in range(chips):
            wet_forward(k).wait()
        partial[...] = dot(mass_ref[...], wet[...].reshape(n_row * per_block, width))
        coded, powers = encode(partial[...])
        for j in range(n_col):
            rs_out[j, 0:per_block, :] = coded[j * per_block : (j + 1) * per_block, :]
            rs_out[j, per_block : per_block + PACKED, :] = powers
        for k in range(1, n_col):
            rs_copy(k).start()
        pressure = partial[pl.ds(pl.multiple_of(my_col * per_block, per_block), per_block), :]
        for k in range(1, n_col):
            rs_copy(k).wait()
        for k in range(1, n_col):
            other = lax.rem(my_col + k, n_col)
            pressure = pressure + decode(
                rs_in[other, 0:per_block, :], rs_in[other, per_block : per_block + PACKED, :]
            )
        ordered = dot(order_out[...], pressure.astype(jnp.bfloat16))
        ret_out[...] = ordered.reshape(n_dev, slots, width).astype(jnp.bfloat16)
        start_all(ret_out, ret_in, ret_send, ret_recv)
        ret_in[me] = ret_out[me]
        for side in range(2):
            halo_copy(side, slot).wait()
        high, low = split(decode(halo[slot, 0, 0:pair, :], halo[slot, 0, pair : pair + PACKED, :]))
        stiff[0:pair, :] += banded(0, 0, high, low)
        high, low = split(decode(halo[slot, 1, 0:pair, :], halo[slot, 1, pair : pair + PACKED, :]))
        stiff[rows - pair : rows, :] += banded(pairs - 1, 2 * pair, high, low)
        wait_all(ret_out, ret_in, ret_send, ret_recv)
        returned = ret_in[...].astype(jnp.float32).reshape(flat, width).astype(jnp.bfloat16)
        image = stiff[...] + dot(place[...], returned)
        alpha = jnp.where(degree_no == 0, 1.0, 2.0).astype(jnp.float32)
        beta = jnp.where(degree_no == 0, 0.0, 1.0).astype(jnp.float32)
        now = cur[...]
        following = (image - centre_ref[...] * now) * (alpha * inverse_ref[...]) - beta * prev[...]
        prev[...] = now
        cur[...] = following

    def filter_pass(outer_no, carry):
        def degree_step(degree_no, inner):
            operate(outer_no * DEGREE + degree_no, degree_no)
            return inner

        lax.fori_loop(0, DEGREE, degree_step, 0)
        now = cur[...]
        sq_out[...] = jnp.sum(now * now, axis=0, keepdims=True)
        target = sq_in.at[outer_no]
        start_all(sq_out, target, sq_send, sq_recv, True)
        sq_in[outer_no, me] = sq_out[...]
        wait_all(sq_out, target, sq_send, sq_recv, True)
        squares = jnp.sum(sq_in[outer_no], axis=0)
        scaled = now / jnp.sqrt(squares / (rows * n_dev) + 1e-06)
        cur[...] = scaled
        prev[...] = scaled
        return carry

    lax.fori_loop(0, OUTER, filter_pass, 0)
    result_ref[...] = cur[...]


def body(mode_block, k_blocks, block_cols, panel_node, added_mass, low_edge, high_edge):
    n_row = lax.axis_size("row")
    n_col = lax.axis_size("col")
    devices = n_row * n_col
    my_row = lax.axis_index("row")
    my_col = lax.axis_index("col")
    linear = my_row * n_col + my_col
    rows_dev, width = mode_block.shape
    block_size = k_blocks.shape[2]
    blocks_dev = rows_dev // block_size
    per_block = panel_node.shape[0] // devices
    most = 2 * ((per_block + devices - 1) // devices)
    slots = (most + SUBLANES - 1) // SUBLANES * SUBLANES
    flat = devices * slots

    panel_rows = panel_node.reshape(devices, per_block)
    source = panel_rows // rows_dev
    within = jnp.arange(per_block)
    earlier = within[None, :] < within[:, None]
    owned = source == linear
    rank = jnp.sum((owned[:, None, :] & earlier[None]).astype(jnp.int32), axis=2)
    hit = owned[:, None, :] & (rank[:, None, :] == jnp.arange(slots)[None, :, None])
    local = panel_rows - linear * rows_dev + 1
    back = jnp.sum(jnp.where(hit, local[:, None, :], 0), axis=2) - 1
    send = back.reshape(n_col, n_row, slots).transpose(1, 0, 2)

    def codes(index):
        mine = lax.dynamic_index_in_dim(source, index, 0, keepdims=False)
        same = mine[:, None] == mine[None, :]
        return mine * slots + jnp.sum((same & earlier).astype(jnp.int32), axis=1)

    in_code = codes(my_col * n_row + my_row)
    out_code = codes(linear)
    pair_base = jnp.arange(blocks_dev)[:, None] // 2 * 2
    relative = block_cols - (linear * blocks_dev - 2) - pair_base

    lower = low_edge.astype(jnp.float32) * 0.25
    upper = high_edge.astype(jnp.float32) * 0.25
    centre = (0.5 * (upper + lower)).reshape(1, width)
    inverse = (1.0 / (0.5 * (upper - lower))).reshape(1, width)

    pair = 2 * block_size
    pairs = rows_dev // pair
    f32, bf16 = jnp.float32, jnp.bfloat16
    vmem = pl.BlockSpec(memory_space=pltpu.VMEM)
    dma = pltpu.SemaphoreType.DMA
    return pl.pallas_call(
        functools.partial(kernel, n_row, n_col),
        out_shape=jax.ShapeDtypeStruct(mode_block.shape, f32),
        in_specs=[pl.BlockSpec(memory_space=pltpu.SMEM)] + [vmem] * 9,
        out_specs=vmem,
        scratch_shapes=[
            pltpu.VMEM((rows_dev, width), f32),
            pltpu.VMEM((rows_dev, width), f32),
            pltpu.VMEM((rows_dev, width), bf16),
            pltpu.VMEM((rows_dev, width), bf16),
            pltpu.VMEM((rows_dev, width), f32),
            pltpu.VMEM((pairs, pair, 3 * pair), bf16),
            pltpu.VMEM((pairs, pair, 3 * pair), bf16),
            pltpu.VMEM((flat, rows_dev), bf16),
            pltpu.VMEM((rows_dev, flat), bf16),
            pltpu.VMEM((per_block, flat), bf16),
            pltpu.VMEM((flat, per_block), bf16),
            pltpu.VMEM((devices, slots, width), bf16),
            pltpu.VMEM((devices, slots, width), bf16),
            pltpu.VMEM((n_row, per_block, width), bf16),
            pltpu.VMEM((n_col * per_block, width), f32),
            pltpu.VMEM((n_col, per_block + PACKED, width), jnp.int16),
            pltpu.VMEM((n_col, per_block + PACKED, width), jnp.int16),
            pltpu.VMEM((devices, slots, width), bf16),
            pltpu.VMEM((devices, slots, width), bf16),
            pltpu.VMEM((2, pair + PACKED, width), jnp.int16),
            pltpu.VMEM((2, 2, pair + PACKED, width), jnp.int16),
            pltpu.VMEM((1, width), f32),
            pltpu.VMEM((OUTER, devices, 1, width), f32),
            dma((2,)),
            dma((2, 2)),
            dma((devices,)),
            dma((devices,)),
            dma((n_row,)),
            dma((n_row,)),
            dma((n_col,)),
            dma((n_col,)),
            dma((devices,)),
            dma((devices,)),
            dma((devices,)),
            dma((devices,)),
        ],
        compiler_params=pltpu.CompilerParams(
            collective_id=0, has_side_effects=True, vmem_limit_bytes=60 * 1024 * 1024
        ),
    )(
        relative,
        mode_block,
        k_blocks,
        send.reshape(flat, 1),
        back.reshape(1, flat),
        in_code.reshape(per_block, 1),
        out_code.reshape(1, per_block),
        added_mass,
        centre,
        inverse,
    )


def solution(mesh):
    placed = (
        P(("row", "col"), None),
        P(("row", "col"), None, None, None),
        P(("row", "col"), None),
        P(),
        P("row", "col"),
        P(),
        P(),
    )
    return jax.shard_map(
        body, mesh=mesh, in_specs=placed, out_specs=P(("row", "col"), None), check_vma=False
    )
```

```python
import functools

import jax
import jax.numpy as jnp
from jax import lax
from jax.experimental import pallas as pl
from jax.experimental.pallas import tpu as pltpu
from jax.sharding import PartitionSpec as P

DEGREE = 3
OUTER = 2
SUBLANES = 8
PACKED = 16
CODE_BITS = 15.0
CHAINS = 2
MESH = pl.DeviceIdType.MESH


def dot(left, right):
    return jnp.dot(left, right, preferred_element_type=jnp.float32)


def split(value):
    high = value.astype(jnp.bfloat16)
    low = (value - high.astype(jnp.float32)).astype(jnp.bfloat16)
    return high, low


def encode(value):
    largest = jnp.maximum(jnp.max(jnp.abs(value), axis=0, keepdims=True), 1e-30)
    power = jnp.ceil(jnp.log2(largest))
    coded = jnp.clip(jnp.round(value * jnp.exp2(CODE_BITS - power)), -32767.0, 32767.0)
    powers = jnp.broadcast_to(power, (PACKED, value.shape[1]))
    return coded.astype(jnp.int32).astype(jnp.int16), powers.astype(jnp.int32).astype(jnp.int16)


def decode(coded, powers):
    power = powers.astype(jnp.int32).astype(jnp.float32)[0:1]
    return coded.astype(jnp.int32).astype(jnp.float32) * jnp.exp2(power - CODE_BITS)


def one_hot(left, right):
    return jnp.where(left == right, 1.0, 0.0).astype(jnp.bfloat16)


def kernel(
    n_row, n_col,
    rel_ref, start_ref, k_ref, send_ref, back_ref, in_ref, out_code_ref, mass_ref,
    centre_ref, inverse_ref, result_ref,
    cur, prev, v_hi, v_lo, stiff, k_hi, k_lo, pick, place, order_in, order_out,
    disp_out, disp_in, wet, partial, rs_out, rs_in, ret_out, ret_in, halo_out, halo, sq_out, sq_in,
    halo_send, halo_recv, disp_send, disp_recv, wet_send, wet_recv,
    rs_send, rs_recv, ret_send, ret_recv, sq_send, sq_recv,
):
    n_dev = n_row * n_col
    my_row = lax.axis_index("row")
    my_col = lax.axis_index("col")
    me = my_row * n_col + my_col
    chains, rows, width = cur.shape
    slots = disp_out.shape[2]
    flat = n_dev * slots
    block = k_ref.shape[2]
    pair = 2 * block
    pairs = rows // pair
    per_block = order_in.shape[0]

    def device(index):
        return (index // n_col, lax.rem(index, n_col))

    barrier = pltpu.get_barrier_semaphore()

    def greet(k, carry):
        pl.semaphore_signal(
            barrier, inc=1, device_id=device(lax.rem(me + k, n_dev)), device_id_type=MESH
        )
        return carry

    lax.fori_loop(1, n_dev, greet, 0)

    shape = (flat, rows)
    pick[...] = one_hot(send_ref[...], lax.broadcasted_iota(jnp.int32, shape, 1))
    place[...] = one_hot(lax.broadcasted_iota(jnp.int32, (rows, flat), 0), back_ref[...])
    order_in[...] = one_hot(in_ref[...], lax.broadcasted_iota(jnp.int32, (per_block, flat), 1))
    order_out[...] = one_hot(
        lax.broadcasted_iota(jnp.int32, (flat, per_block), 0), out_code_ref[...]
    )
    for h in range(chains):
        cur[h] = start_ref[:, h * width : (h + 1) * width]
        prev[h] = start_ref[:, h * width : (h + 1) * width]
    pl.semaphore_wait(barrier, n_dev - 1)

    def exchange(source, target, send, recv, h, k, whole):
        to = lax.rem(me + k, n_dev)
        return pltpu.make_async_remote_copy(
            src_ref=source if whole else source.at[to],
            dst_ref=target.at[me],
            send_sem=send.at[h, k],
            recv_sem=recv.at[h, k],
            device_id=device(to),
            device_id_type=MESH,
        )

    def start_all(source, target, send, recv, h, whole=False):
        def step(k, carry):
            exchange(source, target, send, recv, h, k, whole).start()
            return carry

        lax.fori_loop(1, n_dev, step, 0)

    def wait_all(source, target, send, recv, h, whole=False):
        def step(k, carry):
            exchange(source, target, send, recv, h, k, whole).wait()
            return carry

        lax.fori_loop(1, n_dev, step, 0)

    chips = n_row // 2
    partner = my_row + 1 - 2 * lax.rem(my_row, 2)

    def wet_copy(h, k):
        return pltpu.make_async_remote_copy(
            src_ref=wet.at[h, my_row],
            dst_ref=wet.at[h, my_row],
            send_sem=wet_send.at[h, k],
            recv_sem=wet_recv.at[h, k],
            device_id=(lax.rem(my_row + 2 * k, n_row), my_col),
            device_id_type=MESH,
        )

    def wet_forward(h, k):
        held = wet.at[h, lax.rem(my_row + n_row - 2 * k, n_row)]
        return pltpu.make_async_remote_copy(
            src_ref=held,
            dst_ref=held,
            send_sem=wet_send.at[h, chips + k],
            recv_sem=wet_recv.at[h, chips + k],
            device_id=(partner, my_col),
            device_id_type=MESH,
        )

    def rs_copy(h, k):
        to = lax.rem(my_col + k, n_col)
        return pltpu.make_async_remote_copy(
            src_ref=rs_out.at[h, to],
            dst_ref=rs_in.at[h, my_col],
            send_sem=rs_send.at[h, k],
            recv_sem=rs_recv.at[h, k],
            device_id=(my_row, to),
            device_id_type=MESH,
        )

    def halo_copy(h, side, slot):
        to = lax.rem(me + (1 if side == 0 else n_dev - 1), n_dev)
        return pltpu.make_async_remote_copy(
            src_ref=halo_out.at[h, side],
            dst_ref=halo.at[h, slot, side],
            send_sem=halo_send.at[h, side],
            recv_sem=halo_recv.at[h, slot, side],
            device_id=device(to),
            device_id_type=MESH,
        )

    def banded(q, first, values_hi, values_lo):
        count = values_hi.shape[0]
        window_hi = k_hi[q, :, first : first + count]
        window_lo = k_lo[q, :, first : first + count]
        return (
            dot(window_hi, values_hi) + dot(window_lo, values_hi) + dot(window_hi, values_lo)
        )

    def build_band():
        for q in range(pairs):
            for half in range(2):
                i = 2 * q + half
                for o in range(6):
                    total = jnp.zeros((block, block), jnp.float32)
                    for k in range(k_ref.shape[1]):
                        flag = (rel_ref[i, k] == o).astype(jnp.float32)
                        total = total + k_ref[i, k] * flag
                    high, low = split(total)
                    k_hi[q, half * block : (half + 1) * block, o * block : (o + 1) * block] = high
                    k_lo[q, half * block : (half + 1) * block, o * block : (o + 1) * block] = low

    def columns(h):
        return slice(h * width, (h + 1) * width)

    def rescale(h, outer_no):
        wait_all(sq_out.at[h], sq_in.at[h, outer_no], sq_send, sq_recv, h, True)
        squares = jnp.sum(sq_in[h, outer_no], axis=0)
        scaled = cur[h] / jnp.sqrt(squares / (rows * n_dev) + 1e-06)
        cur[h] = scaled
        prev[h] = scaled

    def dispatch(h, step_no):
        @pl.when((step_no > 0) & (lax.rem(step_no, DEGREE) == 0))
        def _():
            rescale(h, step_no // DEGREE - 1)

        high, low = split(cur[h])
        v_hi[h] = high
        v_lo[h] = low
        chosen = dot(pick[...], v_hi[h])
        disp_out[h] = chosen.reshape(n_dev, slots, width).astype(jnp.bfloat16)
        start_all(disp_out.at[h], disp_in.at[h], disp_send, disp_recv, h)
        for side in range(2):
            edge = cur[h, rows - pair : rows, :] if side == 0 else cur[h, 0:pair, :]
            coded, powers = encode(edge)
            halo_out[h, side, 0:pair, :] = coded
            halo_out[h, side, pair : pair + PACKED, :] = powers
        disp_in[h, me] = disp_out[h, me]
        if h == 0:
            @pl.when(step_no == 0)
            def _():
                build_band()

        for q in range(pairs):
            first = max(q - 1, 0) * pair
            last = min(q + 2, pairs) * pair
            stiff[h, q * pair : (q + 1) * pair, :] = banded(
                q, pair if q == 0 else 0, v_hi[h, first:last, :], v_lo[h, first:last, :]
            )

    def gather(h, step_no):
        wait_all(disp_out.at[h], disp_in.at[h], disp_send, disp_recv, h)
        arrived = disp_in[h].astype(jnp.float32).reshape(flat, width).astype(jnp.bfloat16)
        wet[h, my_row] = dot(order_in[...], arrived).astype(jnp.bfloat16)
        for k in range(1, chips):
            wet_copy(h, k).start()
        wet_forward(h, 0).start()
        for side in range(2):
            halo_copy(h, side, lax.rem(step_no, 2)).start()

    def multiply(h, step_no):
        for k in range(1, chips):
            wet_copy(h, k).wait_recv()
            wet_forward(h, k).start()
        for k in range(1, chips):
            wet_copy(h, k).wait_send()
        for k in range(chips):
            wet_forward(h, k).wait()
        partial[h] = dot(mass_ref[...], wet[h].reshape(n_row * per_block, width))
        coded, powers = encode(partial[h])
        for j in range(n_col):
            rs_out[h, j, 0:per_block, :] = coded[j * per_block : (j + 1) * per_block, :]
            rs_out[h, j, per_block : per_block + PACKED, :] = powers
        for k in range(1, n_col):
            rs_copy(h, k).start()

    def give_back(h, step_no):
        own = pl.ds(pl.multiple_of(my_col * per_block, per_block), per_block)
        pressure = partial[h, own, :]
        for k in range(1, n_col):
            rs_copy(h, k).wait()
        for k in range(1, n_col):
            other = lax.rem(my_col + k, n_col)
            pressure = pressure + decode(
                rs_in[h, other, 0:per_block, :], rs_in[h, other, per_block : per_block + PACKED, :]
            )
        ordered = dot(order_out[...], pressure.astype(jnp.bfloat16))
        ret_out[h] = ordered.reshape(n_dev, slots, width).astype(jnp.bfloat16)
        start_all(ret_out.at[h], ret_in.at[h], ret_send, ret_recv, h)
        ret_in[h, me] = ret_out[h, me]
        slot = lax.rem(step_no, 2)
        for side in range(2):
            halo_copy(h, side, slot).wait()
            edge = decode(halo[h, slot, side, 0:pair, :], halo[h, slot, side, pair : pair + PACKED, :])
            high, low = split(edge)
            if side == 0:
                stiff[h, 0:pair, :] += banded(0, 0, high, low)
            else:
                stiff[h, rows - pair : rows, :] += banded(pairs - 1, 2 * pair, high, low)

    def update(h, step_no):
        wait_all(ret_out.at[h], ret_in.at[h], ret_send, ret_recv, h)
        returned = ret_in[h].astype(jnp.float32).reshape(flat, width).astype(jnp.bfloat16)
        image = stiff[h] + dot(place[...], returned)
        degree_no = lax.rem(step_no, DEGREE)
        alpha = jnp.where(degree_no == 0, 1.0, 2.0).astype(jnp.float32)
        beta = jnp.where(degree_no == 0, 0.0, 1.0).astype(jnp.float32)
        now = cur[h]
        inverse = inverse_ref[:, columns(h)]
        following = (image - centre_ref[:, columns(h)] * now) * (alpha * inverse) - beta * prev[h]
        prev[h] = now
        cur[h] = following

        @pl.when(degree_no == DEGREE - 1)
        def _():
            sq_out[h] = jnp.sum(following * following, axis=0, keepdims=True)
            outer_no = step_no // DEGREE
            start_all(sq_out.at[h], sq_in.at[h, outer_no], sq_send, sq_recv, h, True)
            sq_in[h, outer_no, me] = sq_out[h]

    steps = OUTER * DEGREE

    def both(step_no, carry):
        late = step_no - 1
        dispatch(0, step_no)

        @pl.when(step_no > 0)
        def _():
            give_back(1, late)

        gather(0, step_no)

        @pl.when(step_no > 0)
        def _():
            update(1, late)

        multiply(0, step_no)
        dispatch(1, step_no)
        give_back(0, step_no)
        gather(1, step_no)
        update(0, step_no)
        multiply(1, step_no)
        return carry

    lax.fori_loop(0, steps, both, 0)
    give_back(1, steps - 1)
    rescale(0, OUTER - 1)
    update(1, steps - 1)
    result_ref[:, columns(0)] = cur[0]
    rescale(1, OUTER - 1)
    result_ref[:, columns(1)] = cur[1]


def body(mode_block, k_blocks, block_cols, panel_node, added_mass, low_edge, high_edge):
    n_row = lax.axis_size("row")
    n_col = lax.axis_size("col")
    devices = n_row * n_col
    my_row = lax.axis_index("row")
    my_col = lax.axis_index("col")
    linear = my_row * n_col + my_col
    rows_dev, width = mode_block.shape
    block_size = k_blocks.shape[2]
    blocks_dev = rows_dev // block_size
    per_block = panel_node.shape[0] // devices
    most = 2 * ((per_block + devices - 1) // devices)
    slots = (most + SUBLANES - 1) // SUBLANES * SUBLANES
    flat = devices * slots

    panel_rows = panel_node.reshape(devices, per_block)
    source = panel_rows // rows_dev
    within = jnp.arange(per_block)
    earlier = within[None, :] < within[:, None]
    owned = source == linear
    rank = jnp.sum((owned[:, None, :] & earlier[None]).astype(jnp.int32), axis=2)
    hit = owned[:, None, :] & (rank[:, None, :] == jnp.arange(slots)[None, :, None])
    local = panel_rows - linear * rows_dev + 1
    back = jnp.sum(jnp.where(hit, local[:, None, :], 0), axis=2) - 1
    send = back.reshape(n_col, n_row, slots).transpose(1, 0, 2)

    def codes(index):
        mine = lax.dynamic_index_in_dim(source, index, 0, keepdims=False)
        same = mine[:, None] == mine[None, :]
        return mine * slots + jnp.sum((same & earlier).astype(jnp.int32), axis=1)

    in_code = codes(my_col * n_row + my_row)
    out_code = codes(linear)
    pair_base = jnp.arange(blocks_dev)[:, None] // 2 * 2
    relative = block_cols - (linear * blocks_dev - 2) - pair_base

    lower = low_edge.astype(jnp.float32) * 0.25
    upper = high_edge.astype(jnp.float32) * 0.25
    centre = (0.5 * (upper + lower)).reshape(1, width)
    inverse = (1.0 / (0.5 * (upper - lower))).reshape(1, width)

    pair = 2 * block_size
    pairs = rows_dev // pair
    f32, bf16 = jnp.float32, jnp.bfloat16
    vmem = pl.BlockSpec(memory_space=pltpu.VMEM)
    part = width // CHAINS
    dma = pltpu.SemaphoreType.DMA
    return pl.pallas_call(
        functools.partial(kernel, n_row, n_col),
        out_shape=jax.ShapeDtypeStruct(mode_block.shape, f32),
        in_specs=[pl.BlockSpec(memory_space=pltpu.SMEM)] + [vmem] * 9,
        out_specs=vmem,
        scratch_shapes=[
            pltpu.VMEM((CHAINS, rows_dev, part), f32),
            pltpu.VMEM((CHAINS, rows_dev, part), f32),
            pltpu.VMEM((CHAINS, rows_dev, part), bf16),
            pltpu.VMEM((CHAINS, rows_dev, part), bf16),
            pltpu.VMEM((CHAINS, rows_dev, part), f32),
            pltpu.VMEM((pairs, pair, 3 * pair), bf16),
            pltpu.VMEM((pairs, pair, 3 * pair), bf16),
            pltpu.VMEM((flat, rows_dev), bf16),
            pltpu.VMEM((rows_dev, flat), bf16),
            pltpu.VMEM((per_block, flat), bf16),
            pltpu.VMEM((flat, per_block), bf16),
            pltpu.VMEM((CHAINS, devices, slots, part), bf16),
            pltpu.VMEM((CHAINS, devices, slots, part), bf16),
            pltpu.VMEM((CHAINS, n_row, per_block, part), bf16),
            pltpu.VMEM((CHAINS, n_col * per_block, part), f32),
            pltpu.VMEM((CHAINS, n_col, per_block + PACKED, part), jnp.int16),
            pltpu.VMEM((CHAINS, n_col, per_block + PACKED, part), jnp.int16),
            pltpu.VMEM((CHAINS, devices, slots, part), bf16),
            pltpu.VMEM((CHAINS, devices, slots, part), bf16),
            pltpu.VMEM((CHAINS, 2, pair + PACKED, part), jnp.int16),
            pltpu.VMEM((CHAINS, 2, 2, pair + PACKED, part), jnp.int16),
            pltpu.VMEM((CHAINS, 1, part), f32),
            pltpu.VMEM((CHAINS, OUTER, devices, 1, part), f32),
            dma((CHAINS, 2)),
            dma((CHAINS, 2, 2)),
            dma((CHAINS, devices)),
            dma((CHAINS, devices)),
            dma((CHAINS, n_row)),
            dma((CHAINS, n_row)),
            dma((CHAINS, n_col)),
            dma((CHAINS, n_col)),
            dma((CHAINS, devices)),
            dma((CHAINS, devices)),
            dma((CHAINS, devices)),
            dma((CHAINS, devices)),
        ],
        compiler_params=pltpu.CompilerParams(
            collective_id=0, has_side_effects=True, vmem_limit_bytes=60 * 1024 * 1024
        ),
    )(
        relative,
        mode_block,
        k_blocks,
        send.reshape(flat, 1),
        back.reshape(1, flat),
        in_code.reshape(per_block, 1),
        out_code.reshape(1, per_block),
        added_mass,
        centre,
        inverse,
    )


def solution(mesh):
    placed = (
        P(("row", "col"), None),
        P(("row", "col"), None, None, None),
        P(("row", "col"), None),
        P(),
        P("row", "col"),
        P(),
        P(),
    )
    return jax.shard_map(
        body, mesh=mesh, in_specs=placed, out_specs=P(("row", "col"), None), check_vma=False
    )
```

```python
import functools

import jax
import jax.numpy as jnp
from jax import lax
from jax.experimental import pallas as pl
from jax.experimental.pallas import tpu as pltpu
from jax.sharding import PartitionSpec as P

DEGREE = 3
OUTER = 2
SUBLANES = 8
PACKED = 16
CODE_BITS = 15.0
MESH = pl.DeviceIdType.MESH


def dot(left, right):
    return jnp.dot(left, right, preferred_element_type=jnp.float32)


def split(value):
    high = value.astype(jnp.bfloat16)
    low = (value - high.astype(jnp.float32)).astype(jnp.bfloat16)
    return high, low


def encode(value):
    largest = jnp.maximum(jnp.max(jnp.abs(value), axis=0, keepdims=True), 1e-30)
    power = jnp.ceil(jnp.log2(largest))
    coded = jnp.clip(jnp.round(value * jnp.exp2(CODE_BITS - power)), -32767.0, 32767.0)
    powers = jnp.broadcast_to(power, (PACKED, value.shape[1]))
    return coded.astype(jnp.int32).astype(jnp.int16), powers.astype(jnp.int32).astype(jnp.int16)


def decode(coded, powers):
    power = powers.astype(jnp.int32).astype(jnp.float32)[0:1]
    return coded.astype(jnp.int32).astype(jnp.float32) * jnp.exp2(power - CODE_BITS)


def one_hot(left, right):
    return jnp.where(left == right, 1.0, 0.0).astype(jnp.bfloat16)


def kernel(
    n_row, n_col,
    rel_ref, start_ref, k_ref, send_ref, back_ref, in_ref, out_code_ref, mass_ref,
    centre_ref, inverse_ref, result_ref,
    cur, prev, v_hi, v_lo, stiff, k_hi, k_lo, pick, place, order_in, order_out,
    disp_out, disp_in, wet, rs_out, rs_in, ret_out, ret_in, halo_out, halo, sq_out, sq_in,
    halo_send, halo_recv, disp_send, disp_recv, wet_send, wet_recv,
    rs_send, rs_recv, ret_send, ret_recv, sq_send, sq_recv,
):
    n_dev = n_row * n_col
    my_row = lax.axis_index("row")
    my_col = lax.axis_index("col")
    me = my_row * n_col + my_col
    rows, width = cur.shape
    slots = disp_out.shape[1]
    flat = n_dev * slots
    block = k_ref.shape[2]
    pair = 2 * block
    pairs = rows // pair
    per_block = order_in.shape[0]

    def device(index):
        return (index // n_col, lax.rem(index, n_col))

    barrier = pltpu.get_barrier_semaphore()

    def greet(k, carry):
        pl.semaphore_signal(
            barrier, inc=1, device_id=device(lax.rem(me + k, n_dev)), device_id_type=MESH
        )
        return carry

    lax.fori_loop(1, n_dev, greet, 0)

    shape = (flat, rows)
    pick[...] = one_hot(send_ref[...], lax.broadcasted_iota(jnp.int32, shape, 1))
    place[...] = one_hot(lax.broadcasted_iota(jnp.int32, (rows, flat), 0), back_ref[...])
    order_in[...] = one_hot(in_ref[...], lax.broadcasted_iota(jnp.int32, (per_block, flat), 1))
    order_out[...] = one_hot(
        lax.broadcasted_iota(jnp.int32, (flat, per_block), 0), out_code_ref[...]
    )
    cur[...] = start_ref[...]
    prev[...] = start_ref[...]
    pl.semaphore_wait(barrier, n_dev - 1)

    def exchange(source, target, send, recv, k, whole):
        to = lax.rem(me + k, n_dev)
        return pltpu.make_async_remote_copy(
            src_ref=source if whole else source.at[to],
            dst_ref=target.at[me],
            send_sem=send.at[k],
            recv_sem=recv.at[k],
            device_id=device(to),
            device_id_type=MESH,
        )

    def start_all(source, target, send, recv, whole=False):
        def step(k, carry):
            exchange(source, target, send, recv, k, whole).start()
            return carry

        lax.fori_loop(1, n_dev, step, 0)

    def wait_all(source, target, send, recv, whole=False):
        def step(k, carry):
            exchange(source, target, send, recv, k, whole).wait()
            return carry

        lax.fori_loop(1, n_dev, step, 0)

    chips = n_row // 2
    partner = my_row + 1 - 2 * lax.rem(my_row, 2)

    def wet_copy(k):
        return pltpu.make_async_remote_copy(
            src_ref=wet.at[my_row],
            dst_ref=wet.at[my_row],
            send_sem=wet_send.at[k],
            recv_sem=wet_recv.at[k],
            device_id=(lax.rem(my_row + 2 * k, n_row), my_col),
            device_id_type=MESH,
        )

    def wet_forward(k):
        held = wet.at[lax.rem(my_row + n_row - 2 * k, n_row)]
        return pltpu.make_async_remote_copy(
            src_ref=held,
            dst_ref=held,
            send_sem=wet_send.at[chips + k],
            recv_sem=wet_recv.at[chips + k],
            device_id=(partner, my_col),
            device_id_type=MESH,
        )

    def rs_copy(k):
        to = lax.rem(my_col + k, n_col)
        return pltpu.make_async_remote_copy(
            src_ref=rs_out.at[to],
            dst_ref=rs_in.at[my_col],
            send_sem=rs_send.at[k],
            recv_sem=rs_recv.at[k],
            device_id=(my_row, to),
            device_id_type=MESH,
        )

    def halo_copy(side, slot):
        to = lax.rem(me + (1 if side == 0 else n_dev - 1), n_dev)
        return pltpu.make_async_remote_copy(
            src_ref=halo_out.at[side],
            dst_ref=halo.at[slot, side],
            send_sem=halo_send.at[side],
            recv_sem=halo_recv.at[slot, side],
            device_id=device(to),
            device_id_type=MESH,
        )

    def banded(q, first, values_hi, values_lo):
        count = values_hi.shape[0]
        window_hi = k_hi[q, :, first : first + count]
        window_lo = k_lo[q, :, first : first + count]
        return (
            dot(window_hi, values_hi) + dot(window_lo, values_hi) + dot(window_hi, values_lo)
        )

    def build_band():
        for q in range(pairs):
            for half in range(2):
                i = 2 * q + half
                for o in range(6):
                    total = jnp.zeros((block, block), jnp.float32)
                    for k in range(k_ref.shape[1]):
                        flag = (rel_ref[i, k] == o).astype(jnp.float32)
                        total = total + k_ref[i, k] * flag
                    high, low = split(total)
                    k_hi[q, half * block : (half + 1) * block, o * block : (o + 1) * block] = high
                    k_lo[q, half * block : (half + 1) * block, o * block : (o + 1) * block] = low

    def operate(step_no, degree_no):
        slot = lax.rem(step_no, 2)
        high, low = split(cur[...])
        v_hi[...] = high
        v_lo[...] = low
        chosen = dot(pick[...], v_hi[...])
        disp_out[...] = chosen.reshape(n_dev, slots, width).astype(jnp.bfloat16)
        start_all(disp_out, disp_in, disp_send, disp_recv)
        for side in range(2):
            edge = cur[rows - pair : rows, :] if side == 0 else cur[0:pair, :]
            coded, powers = encode(edge)
            halo_out[side, 0:pair, :] = coded
            halo_out[side, pair : pair + PACKED, :] = powers
        disp_in[me] = disp_out[me]

        @pl.when(step_no == 0)
        def _():
            build_band()

        for q in range(pairs):
            first = max(q - 1, 0) * pair
            last = min(q + 2, pairs) * pair
            stiff[q * pair : (q + 1) * pair, :] = banded(
                q, pair if q == 0 else 0, v_hi[first:last, :], v_lo[first:last, :]
            )
        wait_all(disp_out, disp_in, disp_send, disp_recv)
        arrived = disp_in[...].astype(jnp.float32).reshape(flat, width).astype(jnp.bfloat16)
        wet[my_row] = dot(order_in[...], arrived).astype(jnp.bfloat16)
        for k in range(1, chips):
            wet_copy(k).start()
        wet_forward(0).start()
        for side in range(2):
            halo_copy(side, slot).start()
        for k in range(1, chips):
            wet_copy(k).wait_recv()
            wet_forward(k).start()
        for k in range(1, chips):
            wet_copy(k).wait_send()
        for k in range(chips):
            wet_forward(k).wait()
        gathered = wet[...].reshape(n_row * per_block, width)

        def product(index):
            chunk = pl.ds(pl.multiple_of(index * per_block, per_block), per_block)
            return dot(mass_ref[chunk, :], gathered)

        for k in range(1, n_col):
            other = lax.rem(my_col + k, n_col)
            coded, powers = encode(product(other))
            rs_out[other, 0:per_block, :] = coded
            rs_out[other, per_block : per_block + PACKED, :] = powers
            rs_copy(k).start()
        pressure = product(my_col)
        for k in range(1, n_col):
            rs_copy(k).wait()
        for k in range(1, n_col):
            other = lax.rem(my_col + k, n_col)
            pressure = pressure + decode(
                rs_in[other, 0:per_block, :], rs_in[other, per_block : per_block + PACKED, :]
            )
        ordered = dot(order_out[...], pressure.astype(jnp.bfloat16))
        ret_out[...] = ordered.reshape(n_dev, slots, width).astype(jnp.bfloat16)
        start_all(ret_out, ret_in, ret_send, ret_recv)
        ret_in[me] = ret_out[me]
        for side in range(2):
            halo_copy(side, slot).wait()
        high, low = split(decode(halo[slot, 0, 0:pair, :], halo[slot, 0, pair : pair + PACKED, :]))
        stiff[0:pair, :] += banded(0, 0, high, low)
        high, low = split(decode(halo[slot, 1, 0:pair, :], halo[slot, 1, pair : pair + PACKED, :]))
        stiff[rows - pair : rows, :] += banded(pairs - 1, 2 * pair, high, low)
        wait_all(ret_out, ret_in, ret_send, ret_recv)
        returned = ret_in[...].astype(jnp.float32).reshape(flat, width).astype(jnp.bfloat16)
        image = stiff[...] + dot(place[...], returned)
        alpha = jnp.where(degree_no == 0, 1.0, 2.0).astype(jnp.float32)
        beta = jnp.where(degree_no == 0, 0.0, 1.0).astype(jnp.float32)
        now = cur[...]
        following = (image - centre_ref[...] * now) * (alpha * inverse_ref[...]) - beta * prev[...]
        prev[...] = now
        cur[...] = following

    def filter_pass(outer_no, carry):
        def degree_step(degree_no, inner):
            operate(outer_no * DEGREE + degree_no, degree_no)
            return inner

        lax.fori_loop(0, DEGREE, degree_step, 0)
        now = cur[...]
        sq_out[...] = jnp.sum(now * now, axis=0, keepdims=True)
        target = sq_in.at[outer_no]
        start_all(sq_out, target, sq_send, sq_recv, True)
        sq_in[outer_no, me] = sq_out[...]
        wait_all(sq_out, target, sq_send, sq_recv, True)
        squares = jnp.sum(sq_in[outer_no], axis=0)
        scaled = now / jnp.sqrt(squares / (rows * n_dev) + 1e-06)
        cur[...] = scaled
        prev[...] = scaled
        return carry

    lax.fori_loop(0, OUTER, filter_pass, 0)
    result_ref[...] = cur[...]


def body(mode_block, k_blocks, block_cols, panel_node, added_mass, low_edge, high_edge):
    n_row = lax.axis_size("row")
    n_col = lax.axis_size("col")
    devices = n_row * n_col
    my_row = lax.axis_index("row")
    my_col = lax.axis_index("col")
    linear = my_row * n_col + my_col
    rows_dev, width = mode_block.shape
    block_size = k_blocks.shape[2]
    blocks_dev = rows_dev // block_size
    per_block = panel_node.shape[0] // devices
    most = 2 * ((per_block + devices - 1) // devices)
    slots = (most + SUBLANES - 1) // SUBLANES * SUBLANES
    flat = devices * slots

    panel_rows = panel_node.reshape(devices, per_block)
    source = panel_rows // rows_dev
    within = jnp.arange(per_block)
    earlier = within[None, :] < within[:, None]
    owned = source == linear
    rank = jnp.sum((owned[:, None, :] & earlier[None]).astype(jnp.int32), axis=2)
    hit = owned[:, None, :] & (rank[:, None, :] == jnp.arange(slots)[None, :, None])
    local = panel_rows - linear * rows_dev + 1
    back = jnp.sum(jnp.where(hit, local[:, None, :], 0), axis=2) - 1
    send = back.reshape(n_col, n_row, slots).transpose(1, 0, 2)

    def codes(index):
        mine = lax.dynamic_index_in_dim(source, index, 0, keepdims=False)
        same = mine[:, None] == mine[None, :]
        return mine * slots + jnp.sum((same & earlier).astype(jnp.int32), axis=1)

    in_code = codes(my_col * n_row + my_row)
    out_code = codes(linear)
    pair_base = jnp.arange(blocks_dev)[:, None] // 2 * 2
    relative = block_cols - (linear * blocks_dev - 2) - pair_base

    lower = low_edge.astype(jnp.float32) * 0.25
    upper = high_edge.astype(jnp.float32) * 0.25
    centre = (0.5 * (upper + lower)).reshape(1, width)
    inverse = (1.0 / (0.5 * (upper - lower))).reshape(1, width)

    pair = 2 * block_size
    pairs = rows_dev // pair
    f32, bf16 = jnp.float32, jnp.bfloat16
    vmem = pl.BlockSpec(memory_space=pltpu.VMEM)
    dma = pltpu.SemaphoreType.DMA
    return pl.pallas_call(
        functools.partial(kernel, n_row, n_col),
        out_shape=jax.ShapeDtypeStruct(mode_block.shape, f32),
        in_specs=[pl.BlockSpec(memory_space=pltpu.SMEM)] + [vmem] * 9,
        out_specs=vmem,
        scratch_shapes=[
            pltpu.VMEM((rows_dev, width), f32),
            pltpu.VMEM((rows_dev, width), f32),
            pltpu.VMEM((rows_dev, width), bf16),
            pltpu.VMEM((rows_dev, width), bf16),
            pltpu.VMEM((rows_dev, width), f32),
            pltpu.VMEM((pairs, pair, 3 * pair), bf16),
            pltpu.VMEM((pairs, pair, 3 * pair), bf16),
            pltpu.VMEM((flat, rows_dev), bf16),
            pltpu.VMEM((rows_dev, flat), bf16),
            pltpu.VMEM((per_block, flat), bf16),
            pltpu.VMEM((flat, per_block), bf16),
            pltpu.VMEM((devices, slots, width), bf16),
            pltpu.VMEM((devices, slots, width), bf16),
            pltpu.VMEM((n_row, per_block, width), bf16),
            pltpu.VMEM((n_col, per_block + PACKED, width), jnp.int16),
            pltpu.VMEM((n_col, per_block + PACKED, width), jnp.int16),
            pltpu.VMEM((devices, slots, width), bf16),
            pltpu.VMEM((devices, slots, width), bf16),
            pltpu.VMEM((2, pair + PACKED, width), jnp.int16),
            pltpu.VMEM((2, 2, pair + PACKED, width), jnp.int16),
            pltpu.VMEM((1, width), f32),
            pltpu.VMEM((OUTER, devices, 1, width), f32),
            dma((2,)),
            dma((2, 2)),
            dma((devices,)),
            dma((devices,)),
            dma((n_row,)),
            dma((n_row,)),
            dma((n_col,)),
            dma((n_col,)),
            dma((devices,)),
            dma((devices,)),
            dma((devices,)),
            dma((devices,)),
        ],
        compiler_params=pltpu.CompilerParams(
            collective_id=0, has_side_effects=True, vmem_limit_bytes=60 * 1024 * 1024
        ),
    )(
        relative,
        mode_block,
        k_blocks,
        send.reshape(flat, 1),
        back.reshape(1, flat),
        in_code.reshape(per_block, 1),
        out_code.reshape(1, per_block),
        added_mass,
        centre,
        inverse,
    )


def solution(mesh):
    placed = (
        P(("row", "col"), None),
        P(("row", "col"), None, None, None),
        P(("row", "col"), None),
        P(),
        P("row", "col"),
        P(),
        P(),
    )
    return jax.shard_map(
        body, mesh=mesh, in_specs=placed, out_specs=P(("row", "col"), None), check_vma=False
    )
```
